32 devices in a mesh: inst: 16 (over z, y, x), cells: 2 (over core).
Axes of the slice: x: 2, y: 2, z: 4, core: 2. Of those that a mesh axis runs over, the one named last changes fastest.
Arguments:
- adjoint: float32 [16, 5, 8, 16, 128], P('inst', None, 'cells'), may hold values from -6 to 6
- objective_gradient: float32 [16, 5, 8, 16, 128], P('inst', None, 'cells'), may hold values from -6 to 6
- jacobian: float32 [16, 3, 5, 5, 8, 16, 128], P('inst', None, None, None, 'cells'), may hold values from -2.5 to 2.5
- second_coef: float32 [16, 3, 8, 16, 128], P('inst', None, 'cells'), may hold values from 0.05 to 0.5
- fourth_coef: float32 [16, 3, 8, 16, 128], P('inst', None, 'cells'), may hold values from 0.01 to 0.1
- time_step: float32 [16, 8, 16, 128], P('inst', 'cells'), may hold values from 0.03 to 0.15
- frequency: float32 [1], replicated, may hold values from 0.5 to 1.5
- damping: float32 [1], replicated, may hold values from 0.02 to 0.08
Outputs:
- updated: float32 [16, 5, 8, 16, 128], P('inst', None, 'cells')
The draws below stay inside these ranges and needn't reach their ends.
All inputs are finite; a program needn't handle non-finite values.
Results may differ from the reference program's by a relative error of at most 0.0001.
Values sent between devices are 32-bit elements; how exact they have to be, the bound alone decides.
A program may use at most 64 MiB of HBM per device.

```python
import math
import jax
import jax.numpy as jnp
from jax import lax

INSTANCES = 16
VARS = 5
NY = 16
NZ = 128
NX = 8


def block_scale(own_key, shape, shards, low, largest):
    level = 1.0
    for dim, parts in shards:
        heights = jax.random.uniform(jax.random.fold_in(jax.random.fold_in(own_key, 6), dim), (parts,), jnp.float32, low / len(shards), largest / len(shards))
        level = level * jnp.repeat(jnp.exp(heights), shape[dim] // parts).reshape((-1,) + (1,) * (len(shape) - 1 - dim))
    return level


def gaussian(stream_key, dims, width, bound, split=(), kind=jnp.bfloat16):
    values = width * jax.random.normal(stream_key, dims, jnp.float32)
    if split:
        values = values * block_scale(stream_key, dims, split, -0.22, 0.18)
    return jnp.clip(values, -bound, bound).astype(kind)


def setup_inputs(seed: int = 0) -> dict:
    keys = jax.random.split(jax.random.key(seed), 9)
    return {
        "adjoint": gaussian(keys[0], (INSTANCES, VARS, NX, NY, NZ), 1.0, 6.0, ((0, 16), (2, 2)), jnp.float32),
        "objective_gradient": gaussian(keys[1], (INSTANCES, VARS, NX, NY, NZ), 1.0, 6.0, ((0, 16), (2, 2)), jnp.float32),
        "jacobian": gaussian(keys[2], (INSTANCES, 3, VARS, VARS, NX, NY, NZ), VARS ** -0.5, 2.5, ((0, 16), (4, 2)), jnp.float32),
        "second_coef": jnp.clip(jnp.exp(math.log(0.5) - 2.3025851 * jax.random.uniform(keys[3], (INSTANCES, 3, NX, NY, NZ), jnp.float32) ** block_scale(keys[3], (INSTANCES, 3, NX, NY, NZ), ((0, 16), (2, 2)), -0.2, 0.2)), 0.05, 0.5),
        "fourth_coef": jnp.clip(jnp.exp(math.log(0.1) - 2.3025851 * jax.random.uniform(keys[4], (INSTANCES, 3, NX, NY, NZ), jnp.float32) ** block_scale(keys[4], (INSTANCES, 3, NX, NY, NZ), ((0, 16), (2, 2)), -0.2, 0.2)), 0.01, 0.1),
        "time_step": jnp.clip(jnp.exp(math.log(0.15) - 1.609438 * jax.random.uniform(keys[5], (INSTANCES, NX, NY, NZ), jnp.float32) ** block_scale(keys[5], (INSTANCES, NX, NY, NZ), ((0, 16), (1, 2)), -0.2, 0.2)), 0.03, 0.15),
        "frequency": jnp.clip(jnp.exp(jax.random.uniform(keys[6], (1,), jnp.float32, math.log(0.5), math.log(1.5))), 0.5, 1.5),
        "damping": jnp.clip(jnp.exp(jax.random.uniform(keys[7], (1,), jnp.float32, math.log(0.02), math.log(0.08))), 0.02, 0.08),
    }


def spectral_coupling(frequency_value, damping_value, count):
    positions = jnp.arange(count, dtype=jnp.int32)
    offsets = positions[:, None] - positions[None, :]
    parity = jnp.where(offsets % 2 == 0, 1.0, -1.0).astype(jnp.float32)
    angle = (math.pi / count) * offsets.astype(jnp.float32)
    off_diag = offsets != 0
    sine = jnp.where(off_diag, jnp.sin(angle), 1.0)
    slope = jnp.where(off_diag, 0.5 * parity * jnp.cos(angle) / sine, 0.0)
    curve = jnp.where(off_diag, parity * 0.5 / (sine * sine), count * count / 12.0 + 1.0 / 6.0)
    return (frequency_value * slope + damping_value * curve).astype(jnp.float32)


def face_terms(padded, second_pad, fourth_pad, grid_axis):
    length = padded.shape[grid_axis] - 4

    def cut(source, first, size):
        return lax.slice_in_dim(source, first, first + size, axis=grid_axis)

    jumps = cut(padded, 1, length + 3) - cut(padded, 0, length + 3)
    second_flux = cut(second_pad, 0, length + 3) * jumps
    fourth_flux = cut(fourth_pad, 0, length + 3) * jumps
    divided = cut(fourth_flux, 1, length + 2) - cut(fourth_flux, 0, length + 2)
    central = 0.5 * (cut(padded, 1, length) - cut(padded, 3, length))
    damped = cut(second_flux, 1, length) - cut(second_flux, 2, length)
    damped = damped + cut(divided, 2, length) - 2.0 * cut(divided, 1, length) + cut(divided, 0, length)
    return central, damped


def spatial_one(inputs):
    section_state, jac_one, second_one, fourth_one = inputs
    summed = jnp.zeros_like(section_state)
    for direction in range(3):
        grid_axis = 1 + direction
        widths = [(0, 0), (0, 0), (0, 0), (0, 0)]
        widths[grid_axis] = (2, 2)
        padded = jnp.pad(section_state, widths)
        second_pad = jnp.pad(second_one[direction][None], widths)
        fourth_pad = jnp.pad(fourth_one[direction][None], widths)
        central, damped = face_terms(padded, second_pad, fourth_pad, grid_axis)
        summed = summed + jnp.sum(jac_one[direction] * central[:, None], axis=0) + damped
    return summed


def reference(adjoint, objective_gradient, jacobian, second_coef, fourth_coef, time_step, frequency, damping):
    coupling = spectral_coupling(frequency[0], damping[0], INSTANCES)
    section_state = adjoint
    for section_coef in (0.25, 1.0 / 6.0, 0.375, 0.5, 1.0):
        spatial = lax.map(spatial_one, (section_state, jacobian, second_coef, fourth_coef))
        coupled = jnp.einsum("jk,jvxyz->kvxyz", coupling, section_state, precision=lax.Precision.HIGHEST)
        residual = spatial + coupled + objective_gradient
        section_state = adjoint - section_coef * time_step[:, None] * residual
    return section_state
```

```python
import functools
import math

import jax
import jax.numpy as jnp
from jax import lax
from jax.experimental import pallas as pl
from jax.experimental.pallas import tpu as pltpu
from jax.sharding import PartitionSpec as P

FACTORS = (0.25, 1.0 / 6.0, 0.375, 0.5, 1.0)
PAD = 8
MESH = pl.DeviceIdType.MESH

A_OUT, A_MIX, V1_OUT, U1_OUT, V2_BACK, V2_MIX, V3_OUT, U3_OUT, V4_BACK, V4_MIX = range(10)
UNITS = 10


def coupling_tables(count):
    slope, curve = [0.0], [count * count / 12.0 + 1.0 / 6.0]
    for m in range(1, count):
        parity = 1.0 if m % 2 == 0 else -1.0
        angle = math.pi * m / count
        slope.append(0.5 * parity * math.cos(angle) / math.sin(angle))
        curve.append(0.5 * parity / math.sin(angle) ** 2)
    return slope, curve


def kernel(
    n, cells, adj, grad, jac, c2, c4, dt, freq, damp, out,
    vp, jv, cx, cy, cz, kk, dtv, gv, zz, sx, rx, sdt, rdt, coef,
    loc_sem, ss, rs, dss, drs, hss, hrs, chs, chr_,
):
    nv, lay, ny, nz = adj.shape
    rows = lay * ny // n
    per = ny // rows
    me = lax.axis_index("inst")
    cell = lax.axis_index("cells")
    has_lo = cell > 0
    has_hi = cell < cells - 1
    mid = slice(PAD, PAD + ny)

    local = [
        (adj, vp.at[0, :, 2 : 2 + lay, mid, :]),
        (dt, dtv),
        (c2.at[0], cx.at[0, 2 : 2 + lay]),
        (c4.at[0], cx.at[1, 2 : 2 + lay]),
        (c2.at[1], cy.at[0, :, mid, :]),
        (c4.at[1], cy.at[1, :, mid, :]),
        (c2.at[2], cz.at[0]),
        (c4.at[2], cz.at[1]),
        (grad, gv),
        (jac, jv),
    ]
    local = [pltpu.make_async_copy(s, d, loc_sem.at[i]) for i, (s, d) in enumerate(local)]
    for c in local:
        c.start()

    barrier = pltpu.get_barrier_semaphore()

    @pl.loop(1, n)
    def _(r):
        pl.semaphore_signal(
            barrier, inc=1, device_id={"inst": lax.rem(me + r, n)}, device_id_type=MESH
        )

    @pl.when(has_lo)
    def _():
        pl.semaphore_signal(barrier, inc=1, device_id={"cells": cell - 1}, device_id_type=MESH)

    @pl.when(has_hi)
    def _():
        pl.semaphore_signal(barrier, inc=1, device_id={"cells": cell + 1}, device_id_type=MESH)

    slope, curve = coupling_tables(n)
    for m in range(n):
        value = freq[0] * slope[m] + damp[0] * curve[m]
        coef[m] = value
        coef[m + n] = value
    pads = jnp.zeros((nv, lay, PAD, nz), jnp.float32)
    for s in range(len(FACTORS)):
        vp[s, :, 2 : 2 + lay, 0:PAD, :] = pads
        vp[s, :, 2 : 2 + lay, PAD + ny :, :] = pads
    cy[:, :, 0:PAD, :] = jnp.zeros((2, lay, PAD, nz), jnp.float32)
    cy[:, :, PAD + ny :, :] = jnp.zeros((2, lay, PAD, nz), jnp.float32)

    @pl.when(jnp.logical_not(has_lo))
    def _():
        cx[:, 0:2] = jnp.zeros((2, 2, ny, nz), jnp.float32)
        for s in range(len(FACTORS)):
            vp[s, :, 0:2, mid, :] = jnp.zeros((nv, 2, ny, nz), jnp.float32)

    @pl.when(jnp.logical_not(has_hi))
    def _():
        cx[:, 2 + lay :] = jnp.zeros((2, 2, ny, nz), jnp.float32)
        for s in range(len(FACTORS)):
            vp[s, :, 2 + lay :, mid, :] = jnp.zeros((nv, 2, ny, nz), jnp.float32)

    pl.semaphore_wait(barrier, n - 1 + has_lo.astype(jnp.int32) + has_hi.astype(jnp.int32))

    def chunk(unit, p, slot):
        return pltpu.make_async_remote_copy(
            src_ref=sx.at[unit, p], dst_ref=rx.at[unit, slot],
            send_sem=ss.at[unit, p], recv_sem=rs.at[unit, slot],
            device_id={"inst": p}, device_id_type=MESH,
        )

    def send(unit):
        @pl.loop(1, n)
        def _(r):
            chunk(unit, lax.rem(me + r, n), me).start()

        rx[unit, me] = sx[unit, me]

    def receive(unit):
        @pl.loop(1, n)
        def _(r):
            p = lax.rem(me + r, n)
            chunk(unit, p, p).wait_recv()

    def dt_chunk(p, slot):
        return pltpu.make_async_remote_copy(
            src_ref=sdt.at[p], dst_ref=rdt.at[slot],
            send_sem=dss.at[p], recv_sem=drs.at[slot],
            device_id={"inst": p}, device_id_type=MESH,
        )

    def halo_up(s):
        return pltpu.make_async_remote_copy(
            src_ref=vp.at[s, :, lay : lay + 2, mid, :], dst_ref=vp.at[s, :, 0:2, mid, :],
            send_sem=hss.at[s, 0], recv_sem=hrs.at[s, 0],
            device_id={"cells": cell + 1}, device_id_type=MESH,
        )

    def halo_down(s):
        return pltpu.make_async_remote_copy(
            src_ref=vp.at[s, :, 2:4, mid, :], dst_ref=vp.at[s, :, 2 + lay : 4 + lay, mid, :],
            send_sem=hss.at[s, 1], recv_sem=hrs.at[s, 1],
            device_id={"cells": cell - 1}, device_id_type=MESH,
        )

    coef_up = pltpu.make_async_remote_copy(
        src_ref=cx.at[:, lay : lay + 2], dst_ref=cx.at[:, 0:2],
        send_sem=chs.at[0], recv_sem=chr_.at[0],
        device_id={"cells": cell + 1}, device_id_type=MESH,
    )
    coef_down = pltpu.make_async_remote_copy(
        src_ref=cx.at[:, 2:4], dst_ref=cx.at[:, 2 + lay : 4 + lay],
        send_sem=chs.at[1], recv_sem=chr_.at[1],
        device_id={"cells": cell - 1}, device_id_type=MESH,
    )

    def start_pair(up, down):
        @pl.when(has_hi)
        def _():
            up.start()

        @pl.when(has_lo)
        def _():
            down.start()

    def land_pair(up, down):
        @pl.when(has_lo)
        def _():
            up.wait_recv()

        @pl.when(has_hi)
        def _():
            down.wait_recv()

    def sent_pair(up, down):
        @pl.when(has_hi)
        def _():
            up.wait_send()

        @pl.when(has_lo)
        def _():
            down.wait_send()

    def pieces(body):
        @pl.loop(0, lay)
        def _(x):
            for q in range(per):
                for b in range(nv):
                    body(
                        x, x * per + q, b, slice(b * rows, (b + 1) * rows),
                        slice(q * rows, (q + 1) * rows),
                        slice(PAD + q * rows, PAD + (q + 1) * rows),
                    )

    def pack(s, unit):
        def body(x, d, b, chunk_rows, plain, padded):
            sx[unit, d, chunk_rows, :] = vp[s, b, 2 + x, padded, :]

        pieces(body)

    def unpack(unit, s):
        def body(x, d, b, chunk_rows, plain, padded):
            vp[s, b, 2 + x, padded, :] = rx[unit, d, chunk_rows, :]

        pieces(body)

    def finish(unit, s):
        factor = FACTORS[s - 1]

        def body(x, d, b, chunk_rows, plain, padded):
            vp[s, b, 2 + x, padded, :] = zz[b, x, plain, :] - (factor * dtv[x, plain, :]) * rx[
                unit, d, chunk_rows, :
            ]

        pieces(body)

    lanes = lax.broadcasted_iota(jnp.int32, (ny, nz), 1)
    half_lo = jnp.where(lanes >= 1, 0.5, 0.0)
    half_hi = jnp.where(lanes < nz - 1, 0.5, 0.0)

    def stencil():
        @pl.loop(0, lay)
        def _(x):
            up4 = cx[1, x + 3]
            here3 = 3.0 * cx[1, x + 2] + cx[0, x + 2]
            below3 = 3.0 * cx[1, x + 1] + cx[0, x + 1]
            below4 = cx[1, x]
            kk[0, x] = below4
            kk[1, x] = -(below3 + below4)
            kk[2, x] = -(up4 + here3)
            kk[3, x] = up4
            centre = here3 + below3
            up4 = cy[1, x, PAD + 1 : PAD + 1 + ny, :]
            here3 = 3.0 * cy[1, x, mid, :] + cy[0, x, mid, :]
            low = slice(PAD - 1, PAD - 1 + ny)
            below3 = 3.0 * cy[1, x, low, :] + cy[0, x, low, :]
            below4 = cy[1, x, PAD - 2 : PAD - 2 + ny, :]
            kk[4, x] = below4
            kk[5, x] = -(below3 + below4)
            kk[6, x] = -(up4 + here3)
            kk[7, x] = up4
            centre = centre + here3 + below3
            here4 = cz[1, x]
            here3 = 3.0 * here4 + cz[0, x]
            up4 = jnp.where(lanes < nz - 1, pltpu.roll(here4, nz - 1, 1), 0.0)
            below3 = jnp.where(lanes >= 1, pltpu.roll(here3, 1, 1), 0.0)
            below4 = jnp.where(lanes >= 2, pltpu.roll(here4, 2, 1), 0.0)
            kk[8, x] = below4
            kk[9, x] = jnp.where(lanes >= 1, -(below3 + below4), 0.0)
            kk[10, x] = jnp.where(lanes < nz - 1, -(up4 + here3), 0.0)
            kk[11, x] = jnp.where(lanes < nz - 2, up4, 0.0)
            kk[12, x] = centre + here3 + below3

    def spatial(s, emit):
        factor = FACTORS[s]

        @pl.loop(0, lay)
        def _(x):
            sums, central = [], [[], [], []]
            for b in range(nv):
                v0 = vp[s, b, x + 2, mid, :]
                total = kk[12, x] * v0
                m2, m1 = vp[s, b, x, mid, :], vp[s, b, x + 1, mid, :]
                p1, p2 = vp[s, b, x + 3, mid, :], vp[s, b, x + 4, mid, :]
                total += kk[0, x] * m2 + kk[1, x] * m1 + kk[2, x] * p1 + kk[3, x] * p2
                central[0].append(0.5 * (m1 - p1))
                m2, m1, p1, p2 = (
                    vp[s, b, x + 2, PAD + o : PAD + o + ny, :] for o in (-2, -1, 1, 2)
                )
                total += kk[4, x] * m2 + kk[5, x] * m1 + kk[6, x] * p1 + kk[7, x] * p2
                central[1].append(0.5 * (m1 - p1))
                m2, m1, p1, p2 = (pltpu.roll(v0, o, 1) for o in (2, 1, nz - 1, nz - 2))
                total += kk[8, x] * m2 + kk[9, x] * m1 + kk[10, x] * p1 + kk[11, x] * p2
                central[2].append(half_lo * m1 - half_hi * p1)
                sums.append(total)
            step = factor * dtv[x]
            for b in range(nv):
                total = sums[b] + gv[b, x]
                for d in range(3):
                    for a in range(nv):
                        total += jv[d, a, b, x] * central[d][a]
                emit(x, b, vp[0, b, x + 2, mid, :] - step * total)

    def to_home(x, b, value):
        zz[b, x] = value

    def to_chunks(unit):
        def emit(x, b, value):
            for q in range(per):
                sx[unit, x * per + q, b * rows : (b + 1) * rows, :] = value[
                    q * rows : (q + 1) * rows
                ]

        return emit

    def mix(source, target):
        @pl.loop(0, n)
        def _(k):
            total = coef[n - k] * source(0)
            for j in range(1, n):
                total += coef[n + j - k] * source(j)
            target(k, total)

    local[0].wait()
    pack(0, A_OUT)
    send(A_OUT)
    start_pair(halo_up(0), halo_down(0))
    local[2].wait()
    local[3].wait()
    start_pair(coef_up, coef_down)
    local[1].wait()

    @pl.loop(0, lay)
    def _(x):
        for q in range(per):
            sdt[x * per + q] = dtv[x, q * rows : (q + 1) * rows, :]

    @pl.loop(1, n)
    def _(r):
        dt_chunk(lax.rem(me + r, n), me).start()

    rdt[me] = sdt[me]
    for c in local[4:]:
        c.wait()
    land_pair(coef_up, coef_down)
    stencil()
    land_pair(halo_up(0), halo_down(0))
    spatial(0, to_home)
    receive(A_OUT)

    def store(unit):
        def target(k, value):
            sx[unit, k] = value

        return target

    mix(lambda j: rx[A_OUT, j], store(A_MIX))
    send(A_MIX)

    @pl.loop(1, n)
    def _(r):
        p = lax.rem(me + r, n)
        dt_chunk(p, p).wait_recv()

    receive(A_MIX)
    finish(A_MIX, 1)

    for s, v_out, u_out, v_back, v_mix in (
        (1, V1_OUT, U1_OUT, V2_BACK, V2_MIX),
        (3, V3_OUT, U3_OUT, V4_BACK, V4_MIX),
    ):
        pack(s, v_out)
        start_pair(halo_up(s), halo_down(s))
        send(v_out)
        land_pair(halo_up(s), halo_down(s))
        spatial(s, to_chunks(u_out))
        send(u_out)
        receive(v_out)
        receive(u_out)

        def advance(k, value, s=s, u_out=u_out, v_back=v_back):
            step = FACTORS[s] * rdt[k]
            for b in range(nv):
                part = slice(b * rows, (b + 1) * rows)
                sx[v_back, k, part, :] = rx[u_out, k, part, :] - step * value[part]

        mix(lambda j: rx[v_out, j], advance)
        send(v_back)
        mix(lambda j: sx[v_back, j], store(v_mix))
        send(v_mix)
        receive(v_back)
        unpack(v_back, s + 1)
        start_pair(halo_up(s + 1), halo_down(s + 1))
        land_pair(halo_up(s + 1), halo_down(s + 1))
        spatial(s + 1, to_home)
        receive(v_mix)
        if s + 2 < len(FACTORS):
            finish(v_mix, s + 2)

    def last(x, d, b, chunk_rows, plain, padded):
        out[b, x, plain, :] = zz[b, x, plain, :] - (FACTORS[-1] * dtv[x, plain, :]) * rx[
            V4_MIX, d, chunk_rows, :
        ]

    pieces(last)

    @pl.loop(1, n)
    def _(r):
        p = lax.rem(me + r, n)
        dt_chunk(p, me).wait_send()
        for unit in range(UNITS):
            chunk(unit, p, me).wait_send()

    for s in range(len(FACTORS)):
        sent_pair(halo_up(s), halo_down(s))
    sent_pair(coef_up, coef_down)


def on_device(n, cells, adjoint, grad, jac, c2, c4, dt, freq, damp):
    nv, lay, ny, nz = adjoint.shape[1:]
    rows = lay * ny // n
    assert rows * n == lay * ny and ny % rows == 0 and lay >= 2
    f32 = jnp.float32
    anywhere = pl.BlockSpec(memory_space=pl.ANY)
    scalar = pl.BlockSpec(memory_space=pltpu.SMEM)
    sections = len(FACTORS)
    dma = pltpu.SemaphoreType.DMA
    tall = ny + 2 * PAD
    result = pl.pallas_call(
        functools.partial(kernel, n, cells),
        out_shape=jax.ShapeDtypeStruct(adjoint.shape[1:], f32),
        in_specs=[anywhere] * 6 + [scalar] * 2,
        out_specs=pl.BlockSpec(memory_space=pltpu.VMEM),
        scratch_shapes=[
            pltpu.VMEM((sections, nv, lay + 4, tall, nz), f32),
            pltpu.VMEM(jac.shape[1:], f32),
            pltpu.VMEM((2, lay + 4, ny, nz), f32),
            pltpu.VMEM((2, lay, tall, nz), f32),
            pltpu.VMEM((2, lay, ny, nz), f32),
            pltpu.VMEM((13, lay, ny, nz), f32),
            pltpu.VMEM((lay, ny, nz), f32),
            pltpu.VMEM((nv, lay, ny, nz), f32),
            pltpu.VMEM((nv, lay, ny, nz), f32),
            pltpu.VMEM((UNITS, n, nv * rows, nz), f32),
            pltpu.VMEM((UNITS, n, nv * rows, nz), f32),
            pltpu.VMEM((n, rows, nz), f32),
            pltpu.VMEM((n, rows, nz), f32),
            pltpu.SMEM((2 * n,), f32),
            dma((10,)),
            dma((UNITS, n)),
            dma((UNITS, n)),
            dma((n,)),
            dma((n,)),
            dma((sections, 2)),
            dma((sections, 2)),
            dma((2,)),
            dma((2,)),
        ],
        compiler_params=pltpu.CompilerParams(collective_id=0, has_side_effects=True),
    )(adjoint[0], grad[0], jac[0], c2[0], c4[0], dt[0], freq, damp)
    return result[None]


def solution(mesh):
    placed = (
        P("inst", None, "cells", None, None),
        P("inst", None, "cells", None, None),
        P("inst", None, None, None, "cells", None, None),
        P("inst", None, "cells", None, None),
        P("inst", None, "cells", None, None),
        P("inst", "cells", None, None),
        P(),
        P(),
    )
    return jax.shard_map(
        functools.partial(on_device, mesh.shape["inst"], mesh.shape["cells"]),
        mesh=mesh,
        in_specs=placed,
        out_specs=P("inst", None, "cells", None, None),
        check_vma=False,
    )
```

```python
import functools
import math

import jax
import jax.numpy as jnp
from jax import lax
from jax.experimental import pallas as pl
from jax.experimental.pallas import tpu as pltpu
from jax.sharding import PartitionSpec as P

FACTORS = (0.25, 1.0 / 6.0, 0.375, 0.5, 1.0)
PAD = 8
MESH = pl.DeviceIdType.MESH

A_OUT, A_MIX, V1_OUT, U1_OUT, V2_BACK, V2_MIX, V3_OUT, U3_OUT, V4_BACK, V4_MIX = range(10)
UNITS = 10


def coupling_tables(count):
    slope, curve = [0.0], [count * count / 12.0 + 1.0 / 6.0]
    for m in range(1, count):
        parity = 1.0 if m % 2 == 0 else -1.0
        angle = math.pi * m / count
        slope.append(0.5 * parity * math.cos(angle) / math.sin(angle))
        curve.append(0.5 * parity / math.sin(angle) ** 2)
    return slope, curve


def kernel(
    n, cells, adj, grad, jac, c2, c4, dt, freq_in, damp_in, out,
    vp, jv, cx, cy, cz, kk, dtv, gv, zz, sx, rx, mm, sdt, rdt, coef, freq, damp,
    loc_sem, ss, rs, dss, drs, hss, hrs, chs, chr_,
):
    nv, lay, ny, nz = adj.shape
    rows = lay * ny // n
    per = ny // rows
    me = lax.axis_index("inst")
    cell = lax.axis_index("cells")
    has_lo = cell > 0
    has_hi = cell < cells - 1
    mid = slice(PAD, PAD + ny)

    local = [
        (adj, vp.at[0, :, 2 : 2 + lay, mid, :]),
        (dt, dtv),
        (c2.at[0], cx.at[0, 2 : 2 + lay]),
        (c4.at[0], cx.at[1, 2 : 2 + lay]),
        (c2.at[1], cy.at[0, :, mid, :]),
        (c4.at[1], cy.at[1, :, mid, :]),
        (c2.at[2], cz.at[0]),
        (c4.at[2], cz.at[1]),
        (grad, gv),
        (jac, jv),
        (freq_in, freq),
        (damp_in, damp),
    ]
    local = [pltpu.make_async_copy(s, d, loc_sem.at[i]) for i, (s, d) in enumerate(local)]
    for c in local:
        c.start()

    barrier = pltpu.get_barrier_semaphore()

    @pl.loop(1, n)
    def _(r):
        pl.semaphore_signal(
            barrier, inc=1, device_id={"inst": lax.rem(me + r, n)}, device_id_type=MESH
        )

    @pl.when(has_lo)
    def _():
        pl.semaphore_signal(barrier, inc=1, device_id={"cells": cell - 1}, device_id_type=MESH)

    @pl.when(has_hi)
    def _():
        pl.semaphore_signal(barrier, inc=1, device_id={"cells": cell + 1}, device_id_type=MESH)

    slope, curve = coupling_tables(n)
    local[10].wait()
    local[11].wait()
    for m in range(n):
        value = freq[0] * slope[m] + damp[0] * curve[m]
        coef[m] = value
        coef[m + n] = value
    pads = jnp.zeros((nv, lay, PAD, nz), jnp.float32)
    for s in range(len(FACTORS)):
        vp[s, :, 2 : 2 + lay, 0:PAD, :] = pads
        vp[s, :, 2 : 2 + lay, PAD + ny :, :] = pads
    cy[:, :, 0:PAD, :] = jnp.zeros((2, lay, PAD, nz), jnp.float32)
    cy[:, :, PAD + ny :, :] = jnp.zeros((2, lay, PAD, nz), jnp.float32)

    @pl.when(jnp.logical_not(has_lo))
    def _():
        cx[:, 0:2] = jnp.zeros((2, 2, ny, nz), jnp.float32)
        for s in range(len(FACTORS)):
            vp[s, :, 0:2, mid, :] = jnp.zeros((nv, 2, ny, nz), jnp.float32)

    @pl.when(jnp.logical_not(has_hi))
    def _():
        cx[:, 2 + lay :] = jnp.zeros((2, 2, ny, nz), jnp.float32)
        for s in range(len(FACTORS)):
            vp[s, :, 2 + lay :, mid, :] = jnp.zeros((nv, 2, ny, nz), jnp.float32)

    half = n // 2

    def partner(i):
        own = i // half
        return lax.rem(me // half + 1 + own, 2) * half + lax.rem(
            lax.rem(me, half) + i + own, half
        )

    def chunk(unit, p, slot):
        return pltpu.make_async_remote_copy(
            src_ref=sx.at[unit, p], dst_ref=rx.at[unit, slot],
            send_sem=ss.at[unit, p], recv_sem=rs.at[unit, slot],
            device_id={"inst": p}, device_id_type=MESH,
        )

    def send(unit):
        @pl.loop(0, n - 1)
        def _(i):
            chunk(unit, partner(i), me).start()

        rx[unit, me] = sx[unit, me]

    def receive(unit):
        @pl.loop(1, n)
        def _(r):
            p = lax.rem(me + r, n)
            chunk(unit, p, p).wait_recv()

    def dt_chunk(p, slot):
        return pltpu.make_async_remote_copy(
            src_ref=sdt.at[p], dst_ref=rdt.at[slot],
            send_sem=dss.at[p], recv_sem=drs.at[slot],
            device_id={"inst": p}, device_id_type=MESH,
        )

    def halo_up(s):
        return pltpu.make_async_remote_copy(
            src_ref=vp.at[s, :, lay : lay + 2, mid, :], dst_ref=vp.at[s, :, 0:2, mid, :],
            send_sem=hss.at[s, 0], recv_sem=hrs.at[s, 0],
            device_id={"cells": cell + 1}, device_id_type=MESH,
        )

    def halo_down(s):
        return pltpu.make_async_remote_copy(
            src_ref=vp.at[s, :, 2:4, mid, :], dst_ref=vp.at[s, :, 2 + lay : 4 + lay, mid, :],
            send_sem=hss.at[s, 1], recv_sem=hrs.at[s, 1],
            device_id={"cells": cell - 1}, device_id_type=MESH,
        )

    coef_up = pltpu.make_async_remote_copy(
        src_ref=cx.at[:, lay : lay + 2], dst_ref=cx.at[:, 0:2],
        send_sem=chs.at[0], recv_sem=chr_.at[0],
        device_id={"cells": cell + 1}, device_id_type=MESH,
    )
    coef_down = pltpu.make_async_remote_copy(
        src_ref=cx.at[:, 2:4], dst_ref=cx.at[:, 2 + lay : 4 + lay],
        send_sem=chs.at[1], recv_sem=chr_.at[1],
        device_id={"cells": cell - 1}, device_id_type=MESH,
    )

    def start_pair(up, down):
        @pl.when(has_hi)
        def _():
            up.start()

        @pl.when(has_lo)
        def _():
            down.start()

    def land_pair(up, down):
        @pl.when(has_lo)
        def _():
            up.wait_recv()

        @pl.when(has_hi)
        def _():
            down.wait_recv()

    def sent_pair(up, down):
        @pl.when(has_hi)
        def _():
            up.wait_send()

        @pl.when(has_lo)
        def _():
            down.wait_send()

    def pieces(body):
        @pl.loop(0, lay)
        def _(x):
            for q in range(per):
                for b in range(nv):
                    body(
                        x, x * per + q, b, slice(b * rows, (b + 1) * rows),
                        slice(q * rows, (q + 1) * rows),
                        slice(PAD + q * rows, PAD + (q + 1) * rows),
                    )

    def pack(s, unit):
        def body(x, d, b, chunk_rows, plain, padded):
            sx[unit, d, chunk_rows, :] = vp[s, b, 2 + x, padded, :]

        pieces(body)

    def unpack(unit, s):
        def body(x, d, b, chunk_rows, plain, padded):
            vp[s, b, 2 + x, padded, :] = rx[unit, d, chunk_rows, :]

        pieces(body)

    def finish(unit, s):
        factor = FACTORS[s - 1]

        def body(x, d, b, chunk_rows, plain, padded):
            vp[s, b, 2 + x, padded, :] = zz[b, x, plain, :] - (factor * dtv[x, plain, :]) * rx[
                unit, d, chunk_rows, :
            ]

        pieces(body)

    lanes = lax.broadcasted_iota(jnp.int32, (ny, nz), 1)
    half_lo = jnp.where(lanes >= 1, 0.5, 0.0)
    half_hi = jnp.where(lanes < nz - 1, 0.5, 0.0)

    def stencil():
        @pl.loop(0, lay)
        def _(x):
            up4 = cx[1, x + 3]
            here3 = 3.0 * cx[1, x + 2] + cx[0, x + 2]
            below3 = 3.0 * cx[1, x + 1] + cx[0, x + 1]
            below4 = cx[1, x]
            kk[0, x] = below4
            kk[1, x] = -(below3 + below4)
            kk[2, x] = -(up4 + here3)
            kk[3, x] = up4
            centre = here3 + below3
            up4 = cy[1, x, PAD + 1 : PAD + 1 + ny, :]
            here3 = 3.0 * cy[1, x, mid, :] + cy[0, x, mid, :]
            low = slice(PAD - 1, PAD - 1 + ny)
            below3 = 3.0 * cy[1, x, low, :] + cy[0, x, low, :]
            below4 = cy[1, x, PAD - 2 : PAD - 2 + ny, :]
            kk[4, x] = below4
            kk[5, x] = -(below3 + below4)
            kk[6, x] = -(up4 + here3)
            kk[7, x] = up4
            centre = centre + here3 + below3
            here4 = cz[1, x]
            here3 = 3.0 * here4 + cz[0, x]
            up4 = jnp.where(lanes < nz - 1, pltpu.roll(here4, nz - 1, 1), 0.0)
            below3 = jnp.where(lanes >= 1, pltpu.roll(here3, 1, 1), 0.0)
            below4 = jnp.where(lanes >= 2, pltpu.roll(here4, 2, 1), 0.0)
            kk[8, x] = below4
            kk[9, x] = jnp.where(lanes >= 1, -(below3 + below4), 0.0)
            kk[10, x] = jnp.where(lanes < nz - 1, -(up4 + here3), 0.0)
            kk[11, x] = jnp.where(lanes < nz - 2, up4, 0.0)
            kk[12, x] = centre + here3 + below3

    def spatial(s, emit):
        factor = FACTORS[s]
        both = has_lo.astype(jnp.int32) * has_hi.astype(jnp.int32)
        back = has_lo.astype(jnp.int32) * (1 - both)
        late = (lay - 2) * (1 - both)

        @pl.loop(0, lay)
        def _(i):
            @pl.when(i == late)
            def _():
                land_pair(halo_up(s), halo_down(s))

            x = back * (lay - 1 - i) + (1 - back) * i
            sums, central = [], [[], [], []]
            for b in range(nv):
                v0 = vp[s, b, x + 2, mid, :]
                total = kk[12, x] * v0
                m2, m1 = vp[s, b, x, mid, :], vp[s, b, x + 1, mid, :]
                p1, p2 = vp[s, b, x + 3, mid, :], vp[s, b, x + 4, mid, :]
                total += kk[0, x] * m2 + kk[1, x] * m1 + kk[2, x] * p1 + kk[3, x] * p2
                central[0].append(0.5 * (m1 - p1))
                m2, m1, p1, p2 = (
                    vp[s, b, x + 2, PAD + o : PAD + o + ny, :] for o in (-2, -1, 1, 2)
                )
                total += kk[4, x] * m2 + kk[5, x] * m1 + kk[6, x] * p1 + kk[7, x] * p2
                central[1].append(0.5 * (m1 - p1))
                m2, m1, p1, p2 = (pltpu.roll(v0, o, 1) for o in (2, 1, nz - 1, nz - 2))
                total += kk[8, x] * m2 + kk[9, x] * m1 + kk[10, x] * p1 + kk[11, x] * p2
                central[2].append(half_lo * m1 - half_hi * p1)
                sums.append(total)
            step = factor * dtv[x]
            for b in range(nv):
                total = sums[b] + gv[b, x]
                for d in range(3):
                    for a in range(nv):
                        total += jv[d, a, b, x] * central[d][a]
                emit(x, b, vp[0, b, x + 2, mid, :] - step * total)

    def to_home(x, b, value):
        zz[b, x] = value

    def to_chunks(unit):
        def emit(x, b, value):
            for q in range(per):
                sx[unit, x * per + q, b * rows : (b + 1) * rows, :] = value[
                    q * rows : (q + 1) * rows
                ]

        return emit

    def mixed(source, k):
        total = coef[n - k] * source(0)
        for j in range(1, n):
            total += coef[n + j - k] * source(j)
        return total

    def form_and_send(unit, form):
        @pl.loop(0, n - 1)
        def _(i):
            p = partner(i)
            sx[unit, p] = form(p)

            @pl.when(i > 0)
            def _():
                chunk(unit, partner(i - 1), me).start()

        value = form(me)
        sx[unit, me] = value
        rx[unit, me] = value
        chunk(unit, partner(n - 2), me).start()

    local[0].wait()
    pack(0, A_OUT)
    pl.semaphore_wait(barrier, n - 1 + has_lo.astype(jnp.int32) + has_hi.astype(jnp.int32))
    send(A_OUT)
    start_pair(halo_up(0), halo_down(0))
    local[2].wait()
    local[3].wait()
    start_pair(coef_up, coef_down)
    local[1].wait()

    @pl.loop(0, lay)
    def _(x):
        for q in range(per):
            sdt[x * per + q] = dtv[x, q * rows : (q + 1) * rows, :]

    @pl.loop(1, n)
    def _(r):
        dt_chunk(lax.rem(me + r, n), me).start()

    rdt[me] = sdt[me]
    for c in local[4:10]:
        c.wait()
    land_pair(coef_up, coef_down)
    stencil()
    spatial(0, to_home)
    receive(A_OUT)

    form_and_send(A_MIX, lambda k: mixed(lambda j: rx[A_OUT, j], k))

    @pl.loop(1, n)
    def _(r):
        p = lax.rem(me + r, n)
        dt_chunk(p, p).wait_recv()

    receive(A_MIX)
    finish(A_MIX, 1)

    for s, v_out, u_out, v_back, v_mix in (
        (1, V1_OUT, U1_OUT, V2_BACK, V2_MIX),
        (3, V3_OUT, U3_OUT, V4_BACK, V4_MIX),
    ):
        start_pair(halo_up(s), halo_down(s))
        pack(s, v_out)
        send(v_out)
        spatial(s, to_chunks(u_out))
        send(u_out)
        receive(v_out)

        @pl.loop(0, n)
        def _(k):
            mm[k] = mixed(lambda j: rx[v_out, j], k)

        def advance(k, s=s, u_out=u_out):
            @pl.when(k != me)
            def _():
                chunk(u_out, k, k).wait_recv()

            step = FACTORS[s] * rdt[k]
            return rx[u_out, k] - jnp.concatenate([step] * nv, axis=0) * mm[k]

        form_and_send(v_back, advance)
        form_and_send(v_mix, lambda k: mixed(lambda j: sx[v_back, j], k))
        receive(v_back)
        unpack(v_back, s + 1)
        start_pair(halo_up(s + 1), halo_down(s + 1))
        spatial(s + 1, to_home)
        receive(v_mix)
        if s + 2 < len(FACTORS):
            finish(v_mix, s + 2)

    def last(x, d, b, chunk_rows, plain, padded):
        out[b, x, plain, :] = zz[b, x, plain, :] - (FACTORS[-1] * dtv[x, plain, :]) * rx[
            V4_MIX, d, chunk_rows, :
        ]

    pieces(last)

    @pl.loop(1, n)
    def _(r):
        p = lax.rem(me + r, n)
        dt_chunk(p, me).wait_send()
        for unit in range(UNITS):
            chunk(unit, p, me).wait_send()

    for s in range(len(FACTORS)):
        sent_pair(halo_up(s), halo_down(s))
    sent_pair(coef_up, coef_down)


def on_device(n, cells, adjoint, grad, jac, c2, c4, dt, freq, damp):
    nv, lay, ny, nz = adjoint.shape[1:]
    rows = lay * ny // n
    assert rows * n == lay * ny and ny % rows == 0 and lay >= 2
    f32 = jnp.float32
    anywhere = pl.BlockSpec(memory_space=pl.ANY)
    sections = len(FACTORS)
    dma = pltpu.SemaphoreType.DMA
    tall = ny + 2 * PAD
    result = pl.pallas_call(
        functools.partial(kernel, n, cells),
        out_shape=jax.ShapeDtypeStruct(adjoint.shape[1:], f32),
        in_specs=[anywhere] * 8,
        out_specs=pl.BlockSpec(memory_space=pltpu.VMEM),
        scratch_shapes=[
            pltpu.VMEM((sections, nv, lay + 4, tall, nz), f32),
            pltpu.VMEM(jac.shape[1:], f32),
            pltpu.VMEM((2, lay + 4, ny, nz), f32),
            pltpu.VMEM((2, lay, tall, nz), f32),
            pltpu.VMEM((2, lay, ny, nz), f32),
            pltpu.VMEM((13, lay, ny, nz), f32),
            pltpu.VMEM((lay, ny, nz), f32),
            pltpu.VMEM((nv, lay, ny, nz), f32),
            pltpu.VMEM((nv, lay, ny, nz), f32),
            pltpu.VMEM((UNITS, n, nv * rows, nz), f32),
            pltpu.VMEM((UNITS, n, nv * rows, nz), f32),
            pltpu.VMEM((n, nv * rows, nz), f32),
            pltpu.VMEM((n, rows, nz), f32),
            pltpu.VMEM((n, rows, nz), f32),
            pltpu.SMEM((2 * n,), f32),
            pltpu.SMEM((1,), f32),
            pltpu.SMEM((1,), f32),
            dma((12,)),
            dma((UNITS, n)),
            dma((UNITS, n)),
            dma((n,)),
            dma((n,)),
            dma((sections, 2)),
            dma((sections, 2)),
            dma((2,)),
            dma((2,)),
        ],
        compiler_params=pltpu.CompilerParams(collective_id=0, has_side_effects=True),
    )(adjoint[0], grad[0], jac[0], c2[0], c4[0], dt[0], freq, damp)
    return result[None]


def solution(mesh):
    placed = (
        P("inst", None, "cells", None, None),
        P("inst", None, "cells", None, None),
        P("inst", None, None, None, "cells", None, None),
        P("inst", None, "cells", None, None),
        P("inst", None, "cells", None, None),
        P("inst", "cells", None, None),
        P(),
        P(),
    )
    return jax.shard_map(
        functools.partial(on_device, mesh.shape["inst"], mesh.shape["cells"]),
        mesh=mesh,
        in_specs=placed,
        out_specs=P("inst", None, "cells", None, None),
        check_vma=False,
    )
```
